256 devices in a mesh: grp: 16 (over y, x_hi, core), fsdp: 16 (over z, x_lo).
Axes of the slice: x: 4 (x_hi: 2, x_lo: 2; x = x_hi * 2 + x_lo), y: 4, z: 8, core: 2. Of those that a mesh axis runs over, the one named last changes fastest.
Arguments:
- inputs: bfloat16 [65536, 8192], P(('grp', 'fsdp')), may hold values from -6 to 6
- upstream: bfloat16 [65536, 1024], P(('grp', 'fsdp')), may hold values from -12 to 12
- value_weight: bfloat16 [8192, 1024], P('fsdp'), may hold values from -0.0625 to 0.0625
- adapter_in: bfloat16 [8192, 8], replicated, may hold values from -0.0625 to 0.0625
- adapter_out: bfloat16 [8, 1024], replicated, may hold values from -0.1875 to 0.1875
- sign_seed: int32 [1], replicated, may hold values from 0 to 1073741823
Outputs:
- input_grads: bfloat16 [65536, 8192], P(('grp', 'fsdp'))
- features: float32 [256, 4096], P(('grp', 'fsdp'))
- mean_grad: float32 [73728], P('fsdp')
The draws below stay inside these ranges and needn't reach their ends.
All inputs are finite; a program needn't handle non-finite values.
Results may differ from the reference program's by a relative error of at most 0.005.
Values may be sent and summed in bfloat16 or wider, within the bound.
A program may use at most 128 MiB of HBM per device.

```python
import math
import jax
import jax.numpy as jnp
from jax import lax

D = 8192
KV = 1024
R = 8
PROJ = 4096
TOK_DEV = 256
PAIRS = 256
TOKENS = 65536
NPARAM = 73728


def shard_levels(own_key, shape, shards, low, top_value):
    factor_of = 1.0
    for axis_at, blocks in shards:
        heights = jax.random.uniform(jax.random.fold_in(jax.random.fold_in(own_key, 6), axis_at), (blocks,), jnp.float32, low / len(shards), top_value / len(shards))
        factor_of = factor_of * jnp.repeat(jnp.exp(heights), shape[axis_at] // blocks).reshape((-1,) + (1,) * (len(shape) - 1 - axis_at))
    return factor_of


def gaussian(key, shape, scale, reach, shards=(), kind=jnp.bfloat16):
    result = scale * jax.random.normal(key, shape, jnp.float32)
    if shards:
        result = result * shard_levels(key, shape, shards, -0.22, 0.18)
    return jnp.clip(result, -reach, reach).astype(kind)


def setup_inputs(seed: int = 0) -> dict:
    key_list = jax.random.split(jax.random.key(seed), 7)
    return {
        "inputs": gaussian(key_list[0], (TOKENS, D), 1.0, 6.0, ((0, 256),)),
        "upstream": gaussian(key_list[1], (TOKENS, KV), 2.0, 12.0, ((0, 256),)),
        "value_weight": gaussian(key_list[2], (D, KV), D ** -0.5, 0.0625, ((0, 16),)),
        "adapter_in": gaussian(key_list[3], (D, R), D ** -0.5, 0.0625),
        "adapter_out": gaussian(key_list[4], (R, KV), KV ** -0.5, 0.1875),
        "sign_seed": jax.random.randint(key_list[5], (1,), 0, 1073741824).astype(jnp.int32),
    }


lowrank_scale_factor = 2.0

def contract_last(left, right):
    return lax.dot_general(left, right, (((1,), (1,)), ((), ())), preferred_element_type=jnp.float32)

def leading_contraction(left, right):
    return lax.dot_general(left, right, (((0,), (0,)), ((), ())), preferred_element_type=jnp.float32)

def make_signs(start, count, width, seed_value):
    rows = start + lax.broadcasted_iota(jnp.int32, (count, 1), 0)
    columns = lax.broadcasted_iota(jnp.int32, (1, width), 1)
    mixed = rows * -1640531535 + columns * -2048144789 + seed_value * 668265263
    mixed = mixed ^ mixed >> 15 & 131071
    mixed = mixed * -1028477387
    mixed = mixed ^ mixed >> 13 & 524287
    return (1 - 2 * (mixed >> 16 & 1)).astype(jnp.bfloat16)

def reference(inputs, upstream, value_weight, adapter_in, adapter_out, sign_seed):
    adapter_expanded = adapter_in.astype(jnp.float32)
    pair_inputs = inputs.reshape(PAIRS, TOK_DEV, D)
    pair_upstream = upstream.reshape(PAIRS, TOK_DEV, KV)

    def one_pair(operands):
        rows_in, lifted_rows = operands
        passed_along = contract_last(lifted_rows, adapter_out)
        main_part = contract_last(lifted_rows, value_weight)
        lowrank_portion = jnp.dot(lowrank_scale_factor * passed_along, adapter_expanded.T, precision=lax.Precision.HIGHEST)
        grads_rows = (main_part + lowrank_portion).astype(jnp.bfloat16)
        rescaled_values = (lowrank_scale_factor * passed_along).astype(jnp.bfloat16)
        rank_reduced = jnp.dot(rows_in, adapter_in, preferred_element_type=jnp.float32).astype(jnp.bfloat16)
        grad_in = leading_contraction(rows_in, rescaled_values)
        output_gradient = lowrank_scale_factor * leading_contraction(rank_reduced, lifted_rows)
        flat = jnp.concatenate([grad_in.reshape(-1), output_gradient.reshape(-1)]).astype(jnp.bfloat16)
        return (grads_rows, flat)
    grads_all, pair_grad = lax.map(one_pair, (pair_inputs, pair_upstream))
    input_grads = grads_all.reshape(TOKENS, D)
    block = math.gcd(NPARAM, 4096)
    seed_value = sign_seed[0]

    def add_block(total, block_index):
        offset = block_index * block
        part = lax.dynamic_slice_in_dim(pair_grad, offset, block, 1)
        signs = make_signs(offset, block, PROJ, seed_value)
        return (total + jnp.dot(part, signs, preferred_element_type=jnp.float32), None)
    raw, unused = lax.scan(add_block, jnp.zeros((PAIRS, PROJ), jnp.float32), jnp.arange(NPARAM // block, dtype=jnp.int32))
    features = raw * lax.rsqrt(lax.optimization_barrier(jnp.mean(raw * raw, axis=1, keepdims=True)) + 1e-06)
    mean_grad = lax.optimization_barrier(jnp.sum(pair_grad.astype(jnp.float32), axis=0)) / PAIRS
    return (input_grads, features, mean_grad)
```

```python
import jax
import jax.numpy as jnp
from jax import lax
from jax.experimental import pallas as pl
from jax.experimental.pallas import tpu as pltpu
from jax.sharding import PartitionSpec as P

MESH = pl.DeviceIdType.MESH
F32 = jnp.float32
BF16 = jnp.bfloat16
I32 = jnp.int32

D = 8192
KV = 1024
PROJ = 4096
TOK = 256
SHARD = 512
WIN = 1152
NZ = 8
QUART = 1024
LO, HI = 0, 1
HALF = 96

ROW_MUL = -1640531535
COL_MUL = -2048144789
SEED_MUL = 668265263
MIX_MUL = -1028477387


def nt(left, right, **kw):
    return lax.dot_general(
        left, right, (((1,), (1,)), ((), ())), preferred_element_type=F32, **kw
    )


def nn(left, right, **kw):
    return lax.dot_general(
        left, right, (((1,), (0,)), ((), ())), preferred_element_type=F32, **kw
    )


def kernel(
    x_hbm, u_hbm, w_hbm, ain_ref, aout_ref, seed_ref,
    out_hbm, feat_ref, mean_ref,
    xbuf, ubuf, wbuf, obuf, a3, t3, pbuf, rx, stage, lhs, hb, signs, acc, rsbuf, msum, mrecv, wsum,
    ld_sem, st_sem, zs, zr, xs, xr, ys, yr, cs, cr, p1s, p1r, p2s, p2r, p3s, p3r, ms, mr, rs, rr,
):
    gi = lax.axis_index("grp")
    fi = lax.axis_index("fsdp")
    core = gi % 2
    x_hi = (gi // 2) % 2
    y = gi // 4
    x_lo = fi % 2
    z = fi // 2
    par = y % 2
    xx = x_hi * 2 + x_lo

    def dev(y_, x_, z_, c_):
        return ((y_ * 2 + x_ // 2) * 2 + c_, z_ * 2 + x_ % 2)

    z_up, z_dn = dev(y, xx, (z + 1) % 8, core), dev(y, xx, (z + 7) % 8, core)
    x_up, x_dn = dev(y, (xx + 1) % 4, z, core), dev(y, (xx + 3) % 4, z, core)
    y_up, y_dn = dev((y + 1) % 4, xx, z, core), dev((y + 3) % 4, xx, z, core)
    x_mate = dev(y, x_hi * 2 + (1 - x_lo), z, core)
    c_mate = dev(y, xx, z, 1 - core)

    def member(n):
        zt = (z + n // 4) % 8
        xt = (x_lo + (n // 2) % 2) % 2
        ct = (core + n % 2) % 2
        return zt, xt, ct

    barrier = pltpu.get_barrier_semaphore()

    def signal(target):
        pl.semaphore_signal(barrier, inc=1, device_id=target, device_id_type=MESH)

    def greet(n, carry):
        zt, xt, ct = member(n)
        signal(dev(y, x_hi * 2 + xt, zt, ct))
        return carry

    lax.fori_loop(1, 32, greet, 0)
    for k in range(1, 8):
        g8 = (y * 2 + x_hi + k) % 8
        signal(dev(g8 // 2, (g8 % 2) * 2 + x_lo, z, core))
    signal(dev(y, (xx + 3 + 2 * x_lo) % 4, z, core))

    ld_u = pltpu.make_async_copy(u_hbm, ubuf, ld_sem.at[0])
    ld_u.start()
    ld_x = []
    for k in range(4):
        cols = pl.ds(2048 * k, 2048)
        ld_x.append(pltpu.make_async_copy(x_hbm.at[:, cols], xbuf.at[:, cols], ld_sem.at[1 + k]))
        ld_x[-1].start()
    own_m = fi
    ld_w = pltpu.make_async_copy(w_hbm, wbuf.at[own_m], ld_sem.at[5])
    ld_w.start()

    k0 = QUART * (2 * x_lo + core)
    row16 = lax.broadcasted_iota(I32, (16, QUART), 0)
    col16 = (lax.broadcasted_iota(I32, (16, QUART), 1) + k0) * COL_MUL + seed_ref[0] * SEED_MUL
    hb[0] = row16 * jnp.int32(8) * ROW_MUL + col16
    hb[1] = row16 * ROW_MUL + col16

    ain = ain_ref[...]
    ain_f = ain.astype(F32)
    a3[...] = jnp.concatenate([ain_f, ain_f, ain_f], axis=0).astype(BF16)
    aout = aout_ref[...]
    aout_f = aout.astype(F32)
    aout3 = jnp.concatenate([aout_f, aout_f, aout_f], axis=0).astype(BF16)
    ld_u.wait()
    up = ubuf[...]
    scaled = (2.0 * nt(aout, up)).astype(BF16)
    twice = 2.0 * nt(up, aout3)
    part_hi = twice.astype(BF16)
    rest = twice - part_hi.astype(F32)
    part_mid = rest.astype(BF16)
    part_lo = (rest - part_mid.astype(F32)).astype(BF16)
    lane = lax.broadcasted_iota(I32, (TOK, 24), 1)
    t3[...] = jnp.where(
        lane < 8, part_hi.astype(F32), jnp.where(lane < 16, part_mid.astype(F32), part_lo.astype(F32))
    ).astype(BF16)

    base = core * 256
    win0 = base + 64 * par
    p_own = base + 192 * par
    p_oth = base + 192 * (1 - par)

    def rows(start, n):
        return pl.ds(pl.multiple_of(start, 32), n)

    def half_rows(half):
        return rows(win0 + HALF * half, HALF)

    def shard_at(kind, e):
        return ((z + e) % 8) * 2 + (x_lo if kind == 0 else 1 - x_lo)

    sends = []

    def send(src, dst, s_sem, r_sem, target):
        copy = pltpu.make_async_remote_copy(
            src_ref=src, dst_ref=dst, send_sem=s_sem, recv_sem=r_sem,
            device_id=target, device_id_type=MESH,
        )
        copy.start()
        sends.append(copy)

    def arrive(dst, s_sem, r_sem):
        pltpu.make_async_remote_copy(
            src_ref=dst, dst_ref=dst, send_sem=s_sem, recv_sem=r_sem,
            device_id=c_mate, device_id_type=MESH,
        ).wait_recv()

    def z_send(direction, dz, half, src, m):
        send(
            src, wbuf.at[m, half_rows(half)], zs.at[direction, dz - 1, half],
            zr.at[direction, dz - 1, half], z_up if direction == 0 else z_dn,
        )

    def x_send(e, half, src, m):
        send(src, wbuf.at[m, half_rows(half)], xs.at[e, half], xr.at[e, half], x_up if half == LO else x_dn)

    def z_arrive(direction, dz, half):
        e = (8 - dz) % 8 if direction == 0 else dz
        m = shard_at(0, e)
        ref = wbuf.at[m, half_rows(half)]
        arrive(ref, zs.at[direction, dz - 1, half], zr.at[direction, dz - 1, half])
        last = LO if direction == 0 else HI
        if dz < 3 or (dz == 3 and half == last):
            z_send(direction, dz + 1, half, ref, m)
        x_send(e, half, ref, m)

    def y_send(kind, e):
        m = shard_at(kind, e)
        for j, target in ((0, y_up), (1, y_dn)):
            ref = wbuf.at[m, rows(p_own + 32 * j, 32)]
            send(ref, ref, ys.at[kind, e, j], yr.at[kind, e, j], target)

    def b_arrive(e):
        m = shard_at(1, e)
        for half in (LO, HI):
            arrive(wbuf.at[m, half_rows(half)], xs.at[e, half], xr.at[e, half])
        y_send(1, e)

    def y_arrive(kind, e):
        m = shard_at(kind, e)
        for j in (0, 1):
            arrive(wbuf.at[m, rows(p_oth + 32 * j, 32)], ys.at[kind, e, j], yr.at[kind, e, j])
        ref = wbuf.at[m, rows(base, 256)]
        send(ref, ref, cs.at[kind, e], cr.at[kind, e], c_mate)

    stores = []

    def product(m, h):
        cols = pl.ds(pl.multiple_of(m * SHARD + h * 256, 256), 256)
        part = nt(ubuf[...], wbuf[m, pl.ds(pl.multiple_of(h * 256, 256), 256), :])
        part = part + nn(t3[...], a3[:, cols])
        obuf[m, h] = part.astype(BF16)

    def out_store(m, h, sem):
        cols = pl.ds(pl.multiple_of(m * SHARD + h * 256, 256), 256)
        copy = pltpu.make_async_copy(obuf.at[m, h], out_hbm.at[:, cols], sem)
        copy.start()
        stores.append(copy)

    def shard_product(m, idx):
        @pl.loop(0, 2)
        def _(h):
            product(m, h)

        for h in (0, 1):
            out_store(m, h, st_sem.at[idx, h])

    def c_arrive(kind, e):
        m = shard_at(kind, e)
        arrive(wbuf.at[m, rows((1 - core) * 256, 256)], cs.at[kind, e], cr.at[kind, e])
        shard_product(m, kind * 8 + e)

    def sign_units(first, last):
        @pl.loop(first, last)
        def _(unit):
            r = unit // 9
            blk = unit % 9
            gblk = 9 * z + blk
            is_out = gblk // 64
            i_in = 1024 * gblk + r
            i_out = 65536 - 8192 + 1024 * r + 128 * gblk
            i0 = i_in + is_out * (i_out - i_in)
            step = (8 - 7 * is_out) * 16

            @pl.loop(0, 8, unroll=2)
            def _(g):
                h = hb[is_out] + (i0 + step * g) * ROW_MUL
                h = h ^ lax.shift_right_logical(h, 15)
                h = h * MIX_MUL
                h = (h << 15) ^ (h << 2)
                signs[r, pl.ds(pl.multiple_of(blk * 128 + g * 16, 16), 16), :] = jnp.where(
                    h < 0, -1.0, 1.0
                ).astype(BF16)

    pl.semaphore_wait(barrier, 39)

    for half in (LO, HI):
        z_send(0, 1, half, w_hbm.at[half_rows(half)], own_m)
        z_send(1, 1, 1 - half, w_hbm.at[half_rows(1 - half)], own_m)
        x_send(0, half, w_hbm.at[half_rows(half)], own_m)

    narrow = jnp.zeros((8, TOK), F32)
    for k in range(4):
        ld_x[k].wait()
        cols = pl.ds(2048 * k, 2048)
        chunk = xbuf[:, cols]
        pbuf[:, cols] = nn(scaled, chunk).astype(BF16)
        narrow = narrow + nt(ain[:, 2048 * k : 2048 * k + 2048], chunk)
    pbuf[:, pl.ds(D, KV)] = (2.0 * nn(narrow.astype(BF16), ubuf[...])).astype(BF16)

    own_blk = x_lo * 2 + core
    mate_blk = (1 - x_lo) * 2 + core
    for dz in range(1, 8):
        zt = (z + dz) % 8
        send(
            pbuf.at[:, pl.ds(pl.multiple_of(WIN * zt, 128), WIN)], rx.at[own_blk, z],
            p1s.at[dz], p1r.at[dz], dev(y, xx, zt, core),
        )
    rx[own_blk, z] = pbuf[:, pl.ds(pl.multiple_of(WIN * z, 128), WIN)]

    def stage_two():
        for dz in range(1, 8):
            arrive(rx.at[own_blk, (z + 8 - dz) % 8], p1s.at[dz], p1r.at[dz])
        send(rx.at[own_blk], rx.at[own_blk], p2s.at[0], p2r.at[0], x_mate)
        send(rx.at[own_blk], rx.at[own_blk], p3s.at[0], p3r.at[0], c_mate)

    def stage_three():
        arrive(rx.at[mate_blk], p2s.at[0], p2r.at[0])
        send(rx.at[mate_blk], rx.at[mate_blk], p3s.at[1], p3r.at[1], c_mate)

    g8 = y * 2 + x_hi

    def gather_done():
        arrive(rx.at[x_lo * 2 + 1 - core], p3s.at[0], p3r.at[0])
        arrive(rx.at[(1 - x_lo) * 2 + 1 - core], p3s.at[1], p3r.at[1])
        msum[...] = jnp.zeros_like(msum)

        @pl.loop(0, 32)
        def _(j):
            block = rx[j // 8, j % 8].astype(F32)
            for b in range(9):
                stage[b, pl.ds(pl.multiple_of(j * 8, 8), 8), :] = block[:, 128 * b : 128 * b + 128]
            msum[...] += block

        mrecv[g8] = msum[...]
        for k in range(1, 8):
            t8 = (g8 + k) % 8
            send(
                msum, mrecv.at[g8], ms.at[k], mr.at[k],
                dev(t8 // 2, (t8 % 2) * 2 + x_lo, z, core),
            )
        for r in range(8):
            for b in range(9):
                lhs[r, :, 128 * b : 128 * b + 128] = stage[b, pl.ds(r, 32, stride=8), :].astype(BF16)

    def feature_product():
        acc[...] = jnp.zeros_like(acc)

        @pl.loop(0, 8)
        def _(r):
            acc[...] += nn(lhs[r], signs[r])

        def row_send(n, carry):
            zt, xt, ct = member(n)
            src_row = (xt * 2 + ct) * 8 + zt
            dst_row = (x_lo * 2 + core) * 8 + z
            pltpu.make_async_remote_copy(
                src_ref=acc.at[pl.ds(src_row, 1), :], dst_ref=rsbuf.at[pl.ds(dst_row, 1), :],
                send_sem=rs.at[n], recv_sem=rr.at[n],
                device_id=dev(y, x_hi * 2 + xt, zt, ct), device_id_type=MESH,
            ).start()
            return carry

        lax.fori_loop(1, 32, row_send, 0)
        own_row = pl.ds(own_blk * 8 + z, 1)
        rsbuf[own_row, :] = acc[own_row, :]

    def row_wait(n, carry):
        row = (
            ((x_lo + (n // 2) % 2) % 2) * 2 + (core + n % 2) % 2
        ) * 8 + (z + 8 - n // 4) % 8
        ref = rsbuf.at[pl.ds(row, 1), :]
        copy = pltpu.make_async_remote_copy(
            src_ref=ref, dst_ref=ref, send_sem=rs.at[n], recv_sem=rr.at[n],
            device_id=c_mate, device_id_type=MESH,
        )
        copy.wait_recv()
        copy.wait_send()
        return carry

    def features_done():
        lax.fori_loop(1, 32, row_wait, 0)
        raws = [
            jnp.sum(rsbuf[8 * q : 8 * q + 8, :], axis=0, keepdims=True) for q in range(4)
        ]
        squares = [jnp.sum(raw * raw, axis=1, keepdims=True) for raw in raws]
        mean_sq = (squares[0] + squares[1] + squares[2] + squares[3]) * (1.0 / PROJ)
        scale = lax.rsqrt(mean_sq + 1e-06)
        for q in range(4):
            feat_ref[:, QUART * q : QUART * (q + 1)] = raws[q] * scale

    def mean_done():
        for k in range(1, 8):
            arrive(mrecv.at[(g8 + 8 - k) % 8], ms.at[k], mr.at[k])
        total = mrecv[0]
        for k in range(1, 8):
            total = total + mrecv[k]
        total = total * (1.0 / 256.0)
        wsum[...] = total
        pick = jnp.where(
            lax.broadcasted_iota(I32, (128, 8), 0) % 8 == lax.broadcasted_iota(I32, (128, 8), 1), 1.0, 0.0
        ).astype(F32)
        spread = nn(pick, total, precision=lax.Precision.HIGHEST)
        d_at = lax.broadcasted_iota(I32, (128, WIN), 1)
        lane_at = lax.broadcasted_iota(I32, (128, WIN), 0)
        spread = jnp.where(d_at % 16 == lane_at // 8, spread, 0.0)
        d_row = lax.broadcasted_iota(I32, (40, WIN), 1)
        row_at = lax.broadcasted_iota(I32, (40, WIN), 0)
        chosen = jnp.where(d_row // 16 == row_at + 36 * x_lo, 1.0, 0.0).astype(F32)
        flat = nt(chosen, spread, precision=lax.Precision.HIGHEST)
        mean_ref[...] = flat[:36]

        @pl.when((z == 7) & (x_lo == 0))
        def _():
            for row in range(8, 36):
                g = (row - 8) * 128
                r, b = g // 1024, (g % 1024) // 128
                mean_ref[row : row + 1, :] = wsum[r : r + 1, 128 * (b + 1) : 128 * (b + 2)]

        @pl.when((z == 7) & (x_lo == 1))
        def _():
            for row in range(36):
                g = 3584 + row * 128
                r, b = g // 1024, (g % 1024) // 128
                mean_ref[row : row + 1, :] = wsum[r : r + 1, 128 * (b + 1) : 128 * (b + 2)]

    def tick(k):
        dz = (k + 1) // 2
        half = LO if k % 2 else HI
        z_arrive(0, dz, half)
        z_arrive(1, dz, 1 - half)

    tick(1)
    b_arrive(0)
    sign_units(0, 12)
    stage_two()
    sign_units(12, 24)
    tick(2)
    y_send(0, 7)
    y_send(0, 1)
    sign_units(24, 36)
    stage_three()
    y_arrive(1, 0)
    sign_units(36, 48)
    tick(3)
    b_arrive(7)
    b_arrive(1)
    sign_units(48, 60)
    y_arrive(0, 7)
    y_arrive(0, 1)
    gather_done()
    sign_units(60, 72)
    tick(4)
    y_send(0, 6)
    y_send(0, 2)
    feature_product()
    y_arrive(1, 7)
    y_arrive(1, 1)
    ld_w.wait()
    shard_product(own_m, 0)
    c_arrive(1, 0)
    tick(5)
    b_arrive(6)
    b_arrive(2)
    c_arrive(0, 7)
    c_arrive(0, 1)
    mean_done()
    y_arrive(0, 6)
    y_arrive(0, 2)
    c_arrive(1, 7)
    c_arrive(1, 1)
    tick(6)
    y_send(0, 5)
    y_send(0, 3)
    features_done()
    y_arrive(1, 6)
    y_arrive(1, 2)
    c_arrive(0, 6)
    c_arrive(0, 2)
    tick(7)
    y_send(0, 4)
    b_arrive(5)
    b_arrive(3)
    y_arrive(0, 5)
    y_arrive(0, 3)
    c_arrive(1, 6)
    c_arrive(1, 2)
    y_arrive(0, 4)
    y_arrive(1, 5)
    y_arrive(1, 3)
    c_arrive(0, 5)
    c_arrive(0, 3)
    b_arrive(4)
    c_arrive(0, 4)
    c_arrive(1, 5)
    c_arrive(1, 3)
    y_arrive(1, 4)
    c_arrive(1, 4)

    for copy in sends:
        copy.wait_send()
    for copy in stores:
        copy.wait()


def per_device(inputs, upstream, value_weight, adapter_in, adapter_out, sign_seed):
    any_spec = pl.BlockSpec(memory_space=pl.ANY)
    vmem_spec = pl.BlockSpec(memory_space=pltpu.VMEM)
    dma = pltpu.SemaphoreType.DMA
    grads, features, mean_grad = pl.pallas_call(
        kernel,
        out_shape=(
            jax.ShapeDtypeStruct((TOK, D), BF16),
            jax.ShapeDtypeStruct((1, PROJ), F32),
            jax.ShapeDtypeStruct((36, 128), F32),
        ),
        in_specs=[
            any_spec, any_spec, any_spec, vmem_spec, vmem_spec,
            pl.BlockSpec(memory_space=pltpu.SMEM),
        ],
        out_specs=(any_spec, vmem_spec, vmem_spec),
        scratch_shapes=[
            pltpu.VMEM((TOK, D), BF16),
            pltpu.VMEM((TOK, KV), BF16),
            pltpu.VMEM((16, SHARD, KV), BF16),
            pltpu.VMEM((16, 2, TOK, 256), BF16),
            pltpu.VMEM((24, D), BF16),
            pltpu.VMEM((TOK, 24), BF16),
            pltpu.VMEM((8, D + KV), BF16),
            pltpu.VMEM((4, 8, 8, WIN), BF16),
            pltpu.VMEM((9, 256, 128), F32),
            pltpu.VMEM((8, 32, WIN), BF16),
            pltpu.VMEM((2, 16, QUART), I32),
            pltpu.VMEM((8, WIN, QUART), BF16),
            pltpu.VMEM((32, QUART), F32),
            pltpu.VMEM((32, QUART), F32),
            pltpu.VMEM((8, WIN), F32),
            pltpu.VMEM((8, 8, WIN), F32),
            pltpu.VMEM((8, WIN), F32),
            dma((6,)), dma((16, 2)),
            dma((2, 4, 2)), dma((2, 4, 2)),
            dma((8, 2)), dma((8, 2)),
            dma((2, 8, 2)), dma((2, 8, 2)),
            dma((2, 8)), dma((2, 8)),
            dma((8,)), dma((8,)), dma((1,)), dma((1,)), dma((2,)), dma((2,)),
            dma((8,)), dma((8,)), dma((32,)), dma((32,)),
        ],
        compiler_params=pltpu.CompilerParams(
            collective_id=0, has_side_effects=True, vmem_limit_bytes=64 * 1024 * 1024 - 65536
        ),
    )(inputs, upstream, value_weight, adapter_in.T, adapter_out, sign_seed)
    return grads, features, mean_grad.reshape(-1)


def solution(mesh):
    return jax.shard_map(
        per_device,
        mesh=mesh,
        in_specs=(
            P(("grp", "fsdp"), None),
            P(("grp", "fsdp"), None),
            P("fsdp", None),
            P(),
            P(),
            P(),
        ),
        out_specs=(P(("grp", "fsdp"), None), P(("grp", "fsdp"), None), P("fsdp")),
        check_vma=False,
    )
```

```python
import jax
import jax.numpy as jnp
from jax import lax
from jax.experimental import pallas as pl
from jax.experimental.pallas import tpu as pltpu
from jax.sharding import PartitionSpec as P

MESH = pl.DeviceIdType.MESH
F32 = jnp.float32
BF16 = jnp.bfloat16
I32 = jnp.int32

D = 8192
KV = 1024
PROJ = 4096
TOK = 256
SHARD = 512
WIN = 1152
NZ = 8
QUART = 1024
CHUNK = 64
HALF_TOK = 128

ROW_MUL = -1640531535
COL_MUL = -2048144789
SEED_MUL = 668265263
MIX_MUL_4 = 181057748


def nt(left, right, **kw):
    return lax.dot_general(
        left, right, (((1,), (1,)), ((), ())), preferred_element_type=F32, **kw
    )


def nn(left, right, **kw):
    return lax.dot_general(
        left, right, (((1,), (0,)), ((), ())), preferred_element_type=F32, **kw
    )


def kernel(
    x_hbm, u_hbm, w_hbm, ain_ref, aout_ref, seed_ref,
    out_hbm, feat_ref, mean_ref,
    xbuf, ubuf, wbuf, obuf, a3, t3, aout3, pbuf, rx, stage, lhs, hb, signs, acc, rsbuf, msum, mrecv, mboth, wsum,
    ld_sem, st_sem, us, ur, zs, zr, xs, xr, ys, yr, cs, cr, p1s, p1r, p2s, p2r, p3s, p3r, ms, mr, m2s, m2r, rs, rr,
):
    gi = lax.axis_index("grp")
    fi = lax.axis_index("fsdp")
    core = gi % 2
    x_hi = (gi // 2) % 2
    y = gi // 4
    x_lo = fi % 2
    z = fi // 2
    par = y % 2
    y_hi = y // 2
    xx = x_hi * 2 + x_lo

    def dev(y_, x_, z_, c_):
        return ((y_ * 2 + x_ // 2) * 2 + c_, z_ * 2 + x_ % 2)

    z_up, z_dn = dev(y, xx, (z + 1) % 8, core), dev(y, xx, (z + 7) % 8, core)
    x_up, x_dn = dev(y, (xx + 1) % 4, z, core), dev(y, (xx + 3) % 4, z, core)
    y_up, y_dn = dev((y + 1) % 4, xx, z, core), dev((y + 3) % 4, xx, z, core)
    y_mate = dev(y_hi * 2 + (1 - par), xx, z, core)
    c_mate = dev(y, xx, z, 1 - core)

    def member(n):
        zt = (z + n // 4) % 8
        yt = (par + (n // 2) % 2) % 2
        ct = (core + n % 2) % 2
        return zt, yt, ct

    barrier = pltpu.get_barrier_semaphore()

    def signal(target):
        pl.semaphore_signal(barrier, inc=1, device_id=target, device_id_type=MESH)

    def greet(n, carry):
        zt, yt, ct = member(n)
        signal(dev(y_hi * 2 + yt, xx, zt, ct))
        return carry

    lax.fori_loop(1, 32, greet, 0)
    for k in range(1, 4):
        signal(dev(y, (xx + k) % 4, z, core))
    signal(dev((y + 2) % 4, xx, z, core))
    signal(dev((y + 3 + 2 * par) % 4, xx, z, core))

    ld_u = pltpu.make_async_copy(u_hbm, ubuf.at[pl.ds(0, TOK)], ld_sem.at[0])
    ld_u.start()
    ld_x = []
    for k in range(4):
        cols = pl.ds(2048 * k, 2048)
        ld_x.append(pltpu.make_async_copy(x_hbm.at[:, cols], xbuf.at[:, cols], ld_sem.at[1 + k]))
        ld_x[-1].start()
    ld_w = pltpu.make_async_copy(w_hbm, wbuf.at[z], ld_sem.at[5])
    ld_w.start()

    k0 = QUART * (2 * par + core)
    row16 = lax.broadcasted_iota(I32, (16, QUART), 0)
    col16 = (lax.broadcasted_iota(I32, (16, QUART), 1) + k0) * COL_MUL + seed_ref[0] * SEED_MUL
    hb[0] = row16 * jnp.int32(8) * ROW_MUL + col16
    hb[1] = row16 * ROW_MUL + col16

    ain = ain_ref[...]
    ain_f = ain.astype(F32)
    a3[...] = jnp.concatenate([ain_f, ain_f, ain_f], axis=0).astype(BF16)
    aout = aout_ref[...]
    aout_f = aout.astype(F32)
    aout3[...] = jnp.concatenate([aout_f, aout_f, aout_f], axis=0).astype(BF16)

    def low_rank(first):
        twice = 2.0 * nt(ubuf[first : first + TOK, :], aout3[...])
        part_hi = twice.astype(BF16).astype(F32)
        rest = twice - part_hi
        part_mid = rest.astype(BF16).astype(F32)
        lane = lax.broadcasted_iota(I32, (TOK, 24), 1)
        t3[first : first + TOK, :] = jnp.where(
            lane < 8, part_hi, jnp.where(lane < 16, part_mid, rest - part_mid)
        ).astype(BF16)

    ld_u.wait()
    scaled = (2.0 * nt(aout, ubuf[:TOK, :])).astype(BF16)
    low_rank(0)

    base = core * 256

    def rows(start, n):
        return pl.ds(pl.multiple_of(start, 16), n)

    def chunk_rows(parity, chunk):
        return rows(base + 128 * parity + CHUNK * chunk, CHUNK)

    def shard_at(e):
        return (z + e) % 8

    sends = []

    def send(src, dst, s_sem, r_sem, target):
        copy = pltpu.make_async_remote_copy(
            src_ref=src, dst_ref=dst, send_sem=s_sem, recv_sem=r_sem,
            device_id=target, device_id_type=MESH,
        )
        copy.start()
        sends.append(copy)

    def arrive(dst, s_sem, r_sem):
        pltpu.make_async_remote_copy(
            src_ref=dst, dst_ref=dst, send_sem=s_sem, recv_sem=r_sem,
            device_id=c_mate, device_id_type=MESH,
        ).wait_recv()

    def z_send(direction, dz, chunk, src, m):
        send(
            src, wbuf.at[m, chunk_rows(par, chunk)], zs.at[direction, dz - 1, chunk],
            zr.at[direction, dz - 1, chunk], z_up if direction == 0 else z_dn,
        )

    def z_arrive(direction, dz, chunk):
        e = (8 - dz) % 8 if direction == 0 else dz
        m = shard_at(e)
        ref = wbuf.at[m, chunk_rows(par, chunk)]
        arrive(ref, zs.at[direction, dz - 1, chunk], zr.at[direction, dz - 1, chunk])
        if dz < 3 or (dz == 3 and chunk == direction):
            z_send(direction, dz + 1, chunk, ref, m)
        send(ref, ref, ys.at[e, chunk], yr.at[e, chunk], y_up if chunk == 0 else y_dn)

    def y_arrive(e):
        m = shard_at(e)
        for chunk in (0, 1):
            arrive(wbuf.at[m, chunk_rows(1 - par, chunk)], ys.at[e, chunk], yr.at[e, chunk])
        ref = wbuf.at[m, rows(base, 256)]
        send(ref, ref, cs.at[e], cr.at[e], c_mate)

    stores = []

    def shard_cols(m, lo):
        return pl.ds(pl.multiple_of((m * 2 + lo) * SHARD, SHARD), SHARD)

    def shard_product(e):
        m = shard_at(e)

        @pl.loop(0, 2)
        def _(h):
            start = pl.multiple_of(h * 256, 256)
            cols = pl.ds(pl.multiple_of((m * 2 + x_lo) * SHARD + h * 256, 256), 256)
            part = nt(ubuf[...], wbuf[m, pl.ds(start, 256), :]) + nn(t3[...], a3[:, cols])
            obuf[e, :, pl.ds(start, 256)] = part.astype(BF16)

        cols = shard_cols(m, x_lo)
        for j, target in ((0, x_dn), (1, x_up)):
            send(
                obuf.at[e, pl.ds(TOK + HALF_TOK * j, HALF_TOK), :],
                out_hbm.at[pl.ds(HALF_TOK * j, HALF_TOK), cols], xs.at[e, j], xr.at[e, j], target,
            )
        copy = pltpu.make_async_copy(
            obuf.at[e, pl.ds(0, TOK), :], out_hbm.at[:, cols], st_sem.at[e]
        )
        copy.start()
        stores.append(copy)

    def block_arrive(e):
        cols = shard_cols(shard_at(e), 1 - x_lo)
        for j in (0, 1):
            arrive(out_hbm.at[pl.ds(HALF_TOK * j, HALF_TOK), cols], xs.at[e, j], xr.at[e, j])

    def c_arrive(e):
        arrive(wbuf.at[shard_at(e), rows((1 - core) * 256, 256)], cs.at[e], cr.at[e])
        shard_product(e)

    def tokens_arrive():
        for j in (0, 1):
            arrive(ubuf.at[pl.ds(TOK + HALF_TOK * j, HALF_TOK)], us.at[j], ur.at[j])
        low_rank(TOK)

    def sign_units(first, last):
        @pl.loop(first, last)
        def _(unit):
            r = unit // 9
            blk = unit % 9
            gblk = 9 * z + blk
            is_out = gblk // 64
            i_in = 1024 * gblk + r
            i_out = 65536 - 8192 + 1024 * r + 128 * gblk
            i0 = i_in + is_out * (i_out - i_in)
            step = (8 - 7 * is_out) * 16

            for g in range(8):
                h = hb[is_out] + (i0 + step * g) * ROW_MUL
                h = h ^ lax.shift_right_logical(h, 15)
                h = h * MIX_MUL_4
                h = h ^ (h << 13)
                signs[r, pl.ds(pl.multiple_of(blk * 128 + g * 16, 16), 16), :] = jnp.where(
                    h < 0, -1.0, 1.0
                ).astype(BF16)

    pl.semaphore_wait(barrier, 36)

    for j, target in ((0, x_up), (1, x_dn)):
        send(
            ubuf.at[pl.ds(HALF_TOK * j, HALF_TOK)], ubuf.at[pl.ds(TOK + HALF_TOK * j, HALF_TOK)],
            us.at[j], ur.at[j], target,
        )
    for chunk in (0, 1):
        for direction in (0, 1):
            own = chunk if direction == 0 else 1 - chunk
            z_send(direction, 1, own, w_hbm.at[chunk_rows(par, own)], z)

    narrow = jnp.zeros((8, TOK), F32)
    for k in range(4):
        ld_x[k].wait()
        cols = pl.ds(2048 * k, 2048)
        chunk = xbuf[:, cols]
        pbuf[:, cols] = nn(scaled, chunk).astype(BF16)
        narrow = narrow + nt(ain[:, 2048 * k : 2048 * k + 2048], chunk)
    pbuf[:, pl.ds(D, KV)] = (2.0 * nn(narrow.astype(BF16), ubuf[:TOK, :])).astype(BF16)

    own_blk = par * 2 + core
    mate_blk = (1 - par) * 2 + core
    for dz in (4, 3, 5, 2, 6, 1, 7):
        zt = (z + dz) % 8
        send(
            pbuf.at[:, pl.ds(pl.multiple_of(WIN * zt, 128), WIN)], rx.at[own_blk, z],
            p1s.at[dz], p1r.at[dz], dev(y, xx, zt, core),
        )
    rx[own_blk, z] = pbuf[:, pl.ds(pl.multiple_of(WIN * z, 128), WIN)]

    def stage_two():
        for dz in range(1, 8):
            arrive(rx.at[own_blk, (z + 8 - dz) % 8], p1s.at[dz], p1r.at[dz])
        send(rx.at[own_blk], rx.at[own_blk], p2s.at[0], p2r.at[0], y_mate)
        send(rx.at[own_blk], rx.at[own_blk], p3s.at[0], p3r.at[0], c_mate)

    def stage_three():
        arrive(rx.at[mate_blk], p2s.at[0], p2r.at[0])
        send(rx.at[mate_blk], rx.at[mate_blk], p3s.at[1], p3r.at[1], c_mate)

    def gather_done():
        arrive(rx.at[par * 2 + 1 - core], p3s.at[0], p3r.at[0])
        arrive(rx.at[(1 - par) * 2 + 1 - core], p3s.at[1], p3r.at[1])
        msum[...] = jnp.zeros_like(msum)

        @pl.loop(0, 32)
        def _(j):
            block = rx[j // 8, j % 8].astype(F32)
            for b in range(9):
                stage[b, pl.ds(pl.multiple_of(j * 8, 8), 8), :] = block[:, 128 * b : 128 * b + 128]
            msum[...] += block

        mrecv[xx] = msum[...]
        for k in range(1, 4):
            send(msum, mrecv.at[xx], ms.at[k], mr.at[k], dev(y, (xx + k) % 4, z, core))
        for r in range(8):
            for b in range(9):
                lhs[r, :, 128 * b : 128 * b + 128] = stage[b, pl.ds(r, 32, stride=8), :].astype(BF16)

    def feature_product():
        acc[...] = jnp.zeros_like(acc)

        @pl.loop(0, 8)
        def _(r):
            acc[...] += nn(lhs[r], signs[r])

        def row_send(n, carry):
            zt, yt, ct = member(n)
            src_row = (yt * 2 + ct) * 8 + zt
            dst_row = (par * 2 + core) * 8 + z
            pltpu.make_async_remote_copy(
                src_ref=acc.at[pl.ds(src_row, 1), :], dst_ref=rsbuf.at[pl.ds(dst_row, 1), :],
                send_sem=rs.at[n], recv_sem=rr.at[n],
                device_id=dev(y_hi * 2 + yt, xx, zt, ct), device_id_type=MESH,
            ).start()
            return carry

        lax.fori_loop(1, 32, row_send, 0)
        own_row = pl.ds(own_blk * 8 + z, 1)
        rsbuf[own_row, :] = acc[own_row, :]

    def row_wait(n, carry):
        row = (
            ((par + (n // 2) % 2) % 2) * 2 + (core + n % 2) % 2
        ) * 8 + (z + 8 - n // 4) % 8
        ref = rsbuf.at[pl.ds(row, 1), :]
        copy = pltpu.make_async_remote_copy(
            src_ref=ref, dst_ref=ref, send_sem=rs.at[n], recv_sem=rr.at[n],
            device_id=c_mate, device_id_type=MESH,
        )
        copy.wait_recv()
        copy.wait_send()
        return carry

    def features_done():
        lax.fori_loop(1, 32, row_wait, 0)
        raws = [
            jnp.sum(rsbuf[8 * q : 8 * q + 8, :], axis=0, keepdims=True) for q in range(4)
        ]
        squares = [jnp.sum(raw * raw, axis=1, keepdims=True) for raw in raws]
        mean_sq = (squares[0] + squares[1] + squares[2] + squares[3]) * (1.0 / PROJ)
        scale = lax.rsqrt(mean_sq + 1e-06)
        for q in range(4):
            feat_ref[:, QUART * q : QUART * (q + 1)] = raws[q] * scale

    def mean_half():
        for k in range(1, 4):
            arrive(mrecv.at[(xx + 4 - k) % 4], ms.at[k], mr.at[k])
        mboth[y_hi] = (mrecv[0] + mrecv[1]) + (mrecv[2] + mrecv[3])
        send(mboth.at[y_hi], mboth.at[y_hi], m2s.at[0], m2r.at[0], dev((y + 2) % 4, xx, z, core))

    def mean_done():
        arrive(mboth.at[1 - y_hi], m2s.at[0], m2r.at[0])
        total = mboth[0] + mboth[1]
        total = total * (1.0 / 256.0)
        wsum[...] = total
        pick = jnp.where(
            lax.broadcasted_iota(I32, (128, 8), 0) % 8 == lax.broadcasted_iota(I32, (128, 8), 1), 1.0, 0.0
        ).astype(F32)
        spread = nn(pick, total, precision=lax.Precision.HIGHEST)
        d_at = lax.broadcasted_iota(I32, (128, WIN), 1)
        lane_at = lax.broadcasted_iota(I32, (128, WIN), 0)
        spread = jnp.where(d_at % 16 == lane_at // 8, spread, 0.0)
        d_row = lax.broadcasted_iota(I32, (40, WIN), 1)
        row_at = lax.broadcasted_iota(I32, (40, WIN), 0)
        chosen = jnp.where(d_row // 16 == row_at + 36 * x_lo, 1.0, 0.0).astype(F32)
        flat = nt(chosen, spread, precision=lax.Precision.HIGHEST)
        mean_ref[...] = flat[:36]

        @pl.when((z == 7) & (x_lo == 0))
        def _():
            for row in range(8, 36):
                g = (row - 8) * 128
                r, b = g // 1024, (g % 1024) // 128
                mean_ref[row : row + 1, :] = wsum[r : r + 1, 128 * (b + 1) : 128 * (b + 2)]

        @pl.when((z == 7) & (x_lo == 1))
        def _():
            for row in range(36):
                g = 3584 + row * 128
                r, b = g // 1024, (g % 1024) // 128
                mean_ref[row : row + 1, :] = wsum[r : r + 1, 128 * (b + 1) : 128 * (b + 2)]

    z_arrive(0, 1, 0)
    z_arrive(1, 1, 1)
    sign_units(0, 14)
    z_arrive(0, 1, 1)
    z_arrive(1, 1, 0)
    tokens_arrive()
    ld_w.wait()
    shard_product(0)
    sign_units(14, 34)
    y_arrive(7)
    y_arrive(1)
    stage_two()
    z_arrive(0, 2, 0)
    z_arrive(1, 2, 1)
    c_arrive(7)
    c_arrive(1)
    z_arrive(0, 2, 1)
    z_arrive(1, 2, 0)
    sign_units(34, 56)
    stage_three()
    z_arrive(0, 3, 0)
    z_arrive(1, 3, 1)
    sign_units(56, 72)
    y_arrive(6)
    y_arrive(2)
    z_arrive(0, 3, 1)
    z_arrive(1, 3, 0)
    gather_done()
    c_arrive(6)
    c_arrive(2)
    z_arrive(0, 4, 0)
    z_arrive(1, 4, 1)
    feature_product()
    y_arrive(5)
    y_arrive(3)
    mean_half()
    c_arrive(5)
    c_arrive(3)
    y_arrive(4)
    c_arrive(4)
    features_done()
    mean_done()
    for e in (0, 7, 1, 6, 2, 5, 3, 4):
        block_arrive(e)

    for copy in sends:
        copy.wait_send()
    for copy in stores:
        copy.wait()


def finish(grads_in, feat_in, mean_in, grads_out, feat_out, mean_out, gbuf, fbuf, mbuf, in_sem, out_sem):
    n = 8
    pieces = [
        (grads_in.at[pl.ds(32 * k, 32), :], gbuf.at[pl.ds(32 * k, 32), :], grads_out.at[pl.ds(32 * k, 32), :])
        for k in range(n)
    ]
    pieces.append((feat_in, fbuf, feat_out))
    pieces.append((mean_in, mbuf, mean_out))
    loads = [pltpu.make_async_copy(p[0], p[1], in_sem.at[k]) for k, p in enumerate(pieces)]
    stores = [pltpu.make_async_copy(p[1], p[2], out_sem.at[k]) for k, p in enumerate(pieces)]
    for load in loads:
        load.start()
    for load, store in zip(loads, stores):
        load.wait()
        store.start()
    for store in stores:
        store.wait()


def per_device(inputs, upstream, value_weight, adapter_in, adapter_out, sign_seed):
    any_spec = pl.BlockSpec(memory_space=pl.ANY)
    vmem_spec = pl.BlockSpec(memory_space=pltpu.VMEM)
    dma = pltpu.SemaphoreType.DMA
    grads, features, mean_grad = pl.pallas_call(
        kernel,
        out_shape=(
            jax.ShapeDtypeStruct((TOK, D), BF16),
            jax.ShapeDtypeStruct((1, PROJ), F32),
            jax.ShapeDtypeStruct((36, 128), F32),
        ),
        in_specs=[
            any_spec, any_spec, any_spec, vmem_spec, vmem_spec,
            pl.BlockSpec(memory_space=pltpu.SMEM),
        ],
        out_specs=(any_spec, vmem_spec, vmem_spec),
        scratch_shapes=[
            pltpu.VMEM((TOK, D), BF16),
            pltpu.VMEM((2 * TOK, KV), BF16),
            pltpu.VMEM((8, SHARD, KV), BF16),
            pltpu.VMEM((8, 2 * TOK, SHARD), BF16),
            pltpu.VMEM((24, D), BF16),
            pltpu.VMEM((2 * TOK, 24), BF16),
            pltpu.VMEM((24, KV), BF16),
            pltpu.VMEM((8, D + KV), BF16),
            pltpu.VMEM((4, 8, 8, WIN), BF16),
            pltpu.VMEM((9, 256, 128), F32),
            pltpu.VMEM((8, 32, WIN), BF16),
            pltpu.VMEM((2, 16, QUART), I32),
            pltpu.VMEM((8, WIN, QUART), BF16),
            pltpu.VMEM((32, QUART), F32),
            pltpu.VMEM((32, QUART), F32),
            pltpu.VMEM((8, WIN), F32),
            pltpu.VMEM((4, 8, WIN), F32),
            pltpu.VMEM((2, 8, WIN), F32),
            pltpu.VMEM((8, WIN), F32),
            dma((6,)), dma((8,)), dma((2,)), dma((2,)),
            dma((2, 4, 2)), dma((2, 4, 2)),
            dma((8, 2)), dma((8, 2)),
            dma((8, 2)), dma((8, 2)),
            dma((8,)), dma((8,)),
            dma((8,)), dma((8,)), dma((1,)), dma((1,)), dma((2,)), dma((2,)),
            dma((4,)), dma((4,)), dma((1,)), dma((1,)), dma((32,)), dma((32,)),
        ],
        compiler_params=pltpu.CompilerParams(
            collective_id=0, has_side_effects=True, vmem_limit_bytes=64 * 1024 * 1024 - 65536
        ),
    )(inputs, upstream, value_weight, adapter_in.T, adapter_out, sign_seed)
    grads, features, mean_grad = pl.pallas_call(
        finish,
        out_shape=(
            jax.ShapeDtypeStruct((TOK, D), BF16),
            jax.ShapeDtypeStruct((1, PROJ), F32),
            jax.ShapeDtypeStruct((36, 128), F32),
        ),
        in_specs=[any_spec] * 3,
        out_specs=(any_spec,) * 3,
        scratch_shapes=[
            pltpu.VMEM((TOK, D), BF16), pltpu.VMEM((1, PROJ), F32), pltpu.VMEM((36, 128), F32),
            dma((10,)), dma((10,)),
        ],
    )(grads, features, mean_grad)
    return grads, features, mean_grad.reshape(-1)


def solution(mesh):
    return jax.shard_map(
        per_device,
        mesh=mesh,
        in_specs=(
            P(("grp", "fsdp"), None),
            P(("grp", "fsdp"), None),
            P("fsdp", None),
            P(),
            P(),
            P(),
        ),
        out_specs=(P(("grp", "fsdp"), None), P(("grp", "fsdp"), None), P("fsdp")),
        check_vma=False,
    )
```

```python
import jax
import jax.numpy as jnp
from jax import lax
from jax.experimental import pallas as pl
from jax.experimental.pallas import tpu as pltpu
from jax.sharding import PartitionSpec as P

MESH = pl.DeviceIdType.MESH
F32 = jnp.float32
BF16 = jnp.bfloat16
I32 = jnp.int32

D = 8192
KV = 1024
PROJ = 4096
TOK = 256
SHARD = 512
WIN = 1152
NZ = 8
QUART = 1024
CHUNK = 32
CHUNKS = 4
HALF_TOK = 128

ROW_MUL = -1640531535
COL_MUL = -2048144789
SEED_MUL = 668265263
MIX_MUL_4 = 181057748


def nt(left, right, **kw):
    return lax.dot_general(
        left, right, (((1,), (1,)), ((), ())), preferred_element_type=F32, **kw
    )


def nn(left, right, **kw):
    return lax.dot_general(
        left, right, (((1,), (0,)), ((), ())), preferred_element_type=F32, **kw
    )


def kernel(
    x_hbm, u_hbm, w_hbm, ain_ref, aout_ref, seed_ref,
    out_hbm, feat_ref, mean_ref,
    xbuf, ubuf, wbuf, obuf, a3, t3, aout3, pbuf, rx, stage, lhs, hb, signs, acc, rsbuf, msum, mrecv, mboth, wsum,
    ld_sem, st_sem, us, ur, zs, zr, xs, xr, ys, yr, cs, cr, p1s, p1r, p2s, p2r, p3s, p3r, ms, mr, m2s, m2r, rs, rr,
):
    gi = lax.axis_index("grp")
    fi = lax.axis_index("fsdp")
    core = gi % 2
    x_hi = (gi // 2) % 2
    y = gi // 4
    x_lo = fi % 2
    z = fi // 2
    par = y % 2
    y_hi = y // 2
    xx = x_hi * 2 + x_lo

    def dev(y_, x_, z_, c_):
        return ((y_ * 2 + x_ // 2) * 2 + c_, z_ * 2 + x_ % 2)

    z_up, z_dn = dev(y, xx, (z + 1) % 8, core), dev(y, xx, (z + 7) % 8, core)
    x_up, x_dn = dev(y, (xx + 1) % 4, z, core), dev(y, (xx + 3) % 4, z, core)
    y_up, y_dn = dev((y + 1) % 4, xx, z, core), dev((y + 3) % 4, xx, z, core)
    y_mate = dev(y_hi * 2 + (1 - par), xx, z, core)
    c_mate = dev(y, xx, z, 1 - core)

    def member(n):
        k = n // 4
        dz = 4 + ((k + 1) // 2) * (1 - 2 * (k % 2))
        sub = (n + 1) % 4
        return dz, (par + sub // 2) % 2, (core + sub % 2) % 2

    barrier = pltpu.get_barrier_semaphore()

    def signal(target):
        pl.semaphore_signal(barrier, inc=1, device_id=target, device_id_type=MESH)

    def greet(n, carry):
        dz, yt, ct = member(n)
        signal(dev(y_hi * 2 + yt, xx, (z + dz) % 8, ct))
        return carry

    lax.fori_loop(0, 31, greet, 0)
    for k in range(1, 4):
        signal(dev(y, (xx + k) % 4, z, core))
    signal(dev((y + 2) % 4, xx, z, core))
    signal(dev((y + 3 + 2 * par) % 4, xx, z, core))

    ld_u = pltpu.make_async_copy(u_hbm, ubuf.at[pl.ds(0, TOK)], ld_sem.at[0])
    ld_u.start()
    ld_x = []
    for k in range(4):
        cols = pl.ds(2048 * k, 2048)
        ld_x.append(pltpu.make_async_copy(x_hbm.at[:, cols], xbuf.at[:, cols], ld_sem.at[1 + k]))
        ld_x[-1].start()
    ld_w = pltpu.make_async_copy(w_hbm, wbuf.at[z], ld_sem.at[5])
    ld_w.start()

    k0 = QUART * (2 * par + core)
    row16 = lax.broadcasted_iota(I32, (16, QUART), 0)
    col16 = (lax.broadcasted_iota(I32, (16, QUART), 1) + k0) * COL_MUL + seed_ref[0] * SEED_MUL
    hb[0] = row16 * jnp.int32(8) * ROW_MUL + col16
    hb[1] = row16 * ROW_MUL + col16

    def sign_units(first, last):
        @pl.loop(first, last)
        def _(unit):
            r = unit // 9
            blk = unit % 9
            gblk = 9 * z + blk
            is_out = gblk // 64
            i_in = 1024 * gblk + r
            i_out = 65536 - 8192 + 1024 * r + 128 * gblk
            i0 = i_in + is_out * (i_out - i_in)
            step = (8 - 7 * is_out) * 16

            for g in range(8):
                h = hb[is_out] + (i0 + step * g) * ROW_MUL
                h = h ^ lax.shift_right_logical(h, 15)
                h = h * MIX_MUL_4
                h = h ^ (h << 13)
                signs[r, pl.ds(pl.multiple_of(blk * 128 + g * 16, 16), 16), :] = jnp.where(
                    h < 0, -1.0, 1.0
                ).astype(BF16)

    ain = ain_ref[...]
    ain_f = ain.astype(F32)
    a3[...] = jnp.concatenate([ain_f, ain_f, ain_f], axis=0).astype(BF16)
    aout = aout_ref[...]
    aout_f = aout.astype(F32)
    aout3[...] = jnp.concatenate([aout_f, aout_f, aout_f], axis=0).astype(BF16)

    def low_rank(first):
        twice = 2.0 * nt(ubuf[first : first + TOK, :], aout3[...])
        part_hi = twice.astype(BF16).astype(F32)
        rest = twice - part_hi
        part_mid = rest.astype(BF16).astype(F32)
        lane = lax.broadcasted_iota(I32, (TOK, 24), 1)
        t3[first : first + TOK, :] = jnp.where(
            lane < 8, part_hi, jnp.where(lane < 16, part_mid, rest - part_mid)
        ).astype(BF16)

    ld_u.wait()
    scaled = (2.0 * nt(aout, ubuf[:TOK, :])).astype(BF16)

    base = core * 256

    def rows(start, n):
        return pl.ds(pl.multiple_of(start, 16), n)

    def chunk_rows(parity, chunk):
        return rows(base + 128 * parity + CHUNK * chunk, CHUNK)

    def shard_at(e):
        return (z + e) % 8

    sends = []

    def send(src, dst, s_sem, r_sem, target):
        copy = pltpu.make_async_remote_copy(
            src_ref=src, dst_ref=dst, send_sem=s_sem, recv_sem=r_sem,
            device_id=target, device_id_type=MESH,
        )
        copy.start()
        sends.append(copy)

    def arrive(dst, s_sem, r_sem):
        pltpu.make_async_remote_copy(
            src_ref=dst, dst_ref=dst, send_sem=s_sem, recv_sem=r_sem,
            device_id=c_mate, device_id_type=MESH,
        ).wait_recv()

    def z_send(direction, dz, chunk, src, m):
        send(
            src, wbuf.at[m, chunk_rows(par, chunk)], zs.at[direction, dz - 1, chunk],
            zr.at[direction, dz - 1, chunk], z_up if direction == 0 else z_dn,
        )

    def z_arrive(direction, dz, chunk):
        e = (8 - dz) % 8 if direction == 0 else dz
        m = shard_at(e)
        ref = wbuf.at[m, chunk_rows(par, chunk)]
        arrive(ref, zs.at[direction, dz - 1, chunk], zr.at[direction, dz - 1, chunk])
        if dz < 3 or (dz == 3 and chunk // 2 == direction):
            z_send(direction, dz + 1, chunk, ref, m)
        send(ref, ref, ys.at[e, chunk], yr.at[e, chunk], y_up if chunk < 2 else y_dn)

    def y_arrive(e):
        m = shard_at(e)
        for chunk in range(CHUNKS):
            arrive(wbuf.at[m, chunk_rows(1 - par, chunk)], ys.at[e, chunk], yr.at[e, chunk])
        ref = wbuf.at[m, rows(base, 256)]
        send(ref, ref, cs.at[e], cr.at[e], c_mate)

    stores = []

    def block_cols(m, lo, h):
        return pl.ds(pl.multiple_of((m * 2 + lo) * SHARD + h * 256, 256), 256)

    def block_copy(e, h, j):
        start = pl.multiple_of(h * 256, 256)
        return pltpu.make_async_remote_copy(
            src_ref=obuf.at[e, pl.ds(TOK + HALF_TOK * j, HALF_TOK), pl.ds(start, 256)],
            dst_ref=out_hbm.at[pl.ds(HALF_TOK * j, HALF_TOK), block_cols(shard_at(e), x_lo, h)],
            send_sem=xs.at[e, h, j], recv_sem=xr.at[e, h, j],
            device_id=x_up if j else x_dn, device_id_type=MESH,
        )

    def shard_product(e):
        m = shard_at(e)

        @pl.loop(0, 2)
        def _(h):
            start = pl.multiple_of(h * 256, 256)
            cols = block_cols(m, x_lo, h)
            part = nt(ubuf[...], wbuf[m, pl.ds(start, 256), :]) + nn(t3[...], a3[:, cols])
            obuf[e, :, pl.ds(start, 256)] = part.astype(BF16)
            for j in (0, 1):
                block_copy(e, h, j).start()

        cols = pl.ds(pl.multiple_of((m * 2 + x_lo) * SHARD, SHARD), SHARD)
        copy = pltpu.make_async_copy(
            obuf.at[e, pl.ds(0, TOK), :], out_hbm.at[:, cols], st_sem.at[e]
        )
        copy.start()
        stores.append(copy)

    def block_arrive(e):
        m = shard_at(e)
        for h in (0, 1):
            for j in (0, 1):
                rows_j = pl.ds(HALF_TOK * j, HALF_TOK)
                arrive(out_hbm.at[rows_j, block_cols(m, 1 - x_lo, h)], xs.at[e, h, j], xr.at[e, h, j])
                block_copy(e, h, j).wait_send()

    def c_arrive(e):
        arrive(wbuf.at[shard_at(e), rows((1 - core) * 256, 256)], cs.at[e], cr.at[e])
        shard_product(e)

    def tokens_arrive():
        for j in (0, 1):
            arrive(ubuf.at[pl.ds(TOK + HALF_TOK * j, HALF_TOK)], us.at[j], ur.at[j])
        low_rank(TOK)

    pl.semaphore_wait(barrier, 36)

    for j, target in ((0, x_up), (1, x_dn)):
        send(
            ubuf.at[pl.ds(HALF_TOK * j, HALF_TOK)], ubuf.at[pl.ds(TOK + HALF_TOK * j, HALF_TOK)],
            us.at[j], ur.at[j], target,
        )
    for chunk in range(CHUNKS):
        for direction in (0, 1):
            own = chunk if direction == 0 else CHUNKS - 1 - chunk
            z_send(direction, 1, own, w_hbm.at[chunk_rows(par, own)], z)

    narrow = jnp.zeros((8, TOK), F32)
    for k in range(4):
        ld_x[k].wait()
        cols = pl.ds(2048 * k, 2048)
        chunk = xbuf[:, cols]
        pbuf[:, cols] = nn(scaled, chunk).astype(BF16)
        narrow = narrow + nt(ain[:, 2048 * k : 2048 * k + 2048], chunk)
    pbuf[:, pl.ds(D, KV)] = (2.0 * nn(narrow.astype(BF16), ubuf[:TOK, :])).astype(BF16)

    own_blk = par * 2 + core
    mate_blk = (1 - par) * 2 + core
    for dz in (1, 7, 2, 6, 4, 3, 5):
        zt = (z + dz) % 8
        send(
            pbuf.at[:, pl.ds(pl.multiple_of(WIN * zt, 128), WIN)], rx.at[own_blk, z],
            p1s.at[dz], p1r.at[dz], dev(y, xx, zt, core),
        )
    rx[own_blk, z] = pbuf[:, pl.ds(pl.multiple_of(WIN * z, 128), WIN)]
    low_rank(0)

    def pass_on(slot, n):
        ref = rx.at[own_blk, slot]
        send(ref, ref, p2s.at[n], p2r.at[n], y_mate)
        send(ref, ref, p3s.at[0, n], p3r.at[0, n], c_mate)

    def windows_arrive(distances):
        for dz in distances:
            slot = (z + 8 - dz) % 8
            arrive(rx.at[own_blk, slot], p1s.at[dz], p1r.at[dz])
            pass_on(slot, dz)

    def stage_three():
        for dz in range(8):
            ref = rx.at[mate_blk, (z + 8 - dz) % 8]
            arrive(ref, p2s.at[dz], p2r.at[dz])
        send(rx.at[mate_blk], rx.at[mate_blk], p3s.at[1, 0], p3r.at[1, 0], c_mate)

    def gather_done():
        for dz in range(8):
            arrive(rx.at[par * 2 + 1 - core, (z + 8 - dz) % 8], p3s.at[0, dz], p3r.at[0, dz])
        arrive(rx.at[(1 - par) * 2 + 1 - core], p3s.at[1, 0], p3r.at[1, 0])
        msum[...] = jnp.zeros_like(msum)

        @pl.loop(0, 32)
        def _(j):
            block = rx[j // 8, j % 8].astype(F32)
            for b in range(9):
                stage[b, pl.ds(pl.multiple_of(j * 8, 8), 8), :] = block[:, 128 * b : 128 * b + 128]
            msum[...] += block

        mrecv[xx] = msum[...]
        for k in range(1, 4):
            send(msum, mrecv.at[xx], ms.at[k], mr.at[k], dev(y, (xx + k) % 4, z, core))
        for r in range(8):
            for b in range(9):
                lhs[r, :, 128 * b : 128 * b + 128] = stage[b, pl.ds(r, 32, stride=8), :].astype(BF16)

    def feature_product():
        acc[...] = jnp.zeros_like(acc)

        @pl.loop(0, 8)
        def _(r):
            acc[...] += nn(lhs[r], signs[r])

        def row_send(n, carry):
            dz, yt, ct = member(n)
            zt = (z + dz) % 8
            src_row = (yt * 2 + ct) * 8 + zt
            dst_row = (par * 2 + core) * 8 + z
            pltpu.make_async_remote_copy(
                src_ref=acc.at[pl.ds(src_row, 1), :], dst_ref=rsbuf.at[pl.ds(dst_row, 1), :],
                send_sem=rs.at[n], recv_sem=rr.at[n],
                device_id=dev(y_hi * 2 + yt, xx, zt, ct), device_id_type=MESH,
            ).start()
            return carry

        lax.fori_loop(0, 31, row_send, 0)
        own_row = pl.ds(own_blk * 8 + z, 1)
        rsbuf[own_row, :] = acc[own_row, :]

    def row_wait(n, carry):
        dz, yt, ct = member(n)
        row = (yt * 2 + ct) * 8 + (z + 8 - dz) % 8
        ref = rsbuf.at[pl.ds(row, 1), :]
        copy = pltpu.make_async_remote_copy(
            src_ref=ref, dst_ref=ref, send_sem=rs.at[n], recv_sem=rr.at[n],
            device_id=c_mate, device_id_type=MESH,
        )
        copy.wait_recv()
        copy.wait_send()
        return carry

    def features_done():
        lax.fori_loop(0, 31, row_wait, 0)
        raws = [
            jnp.sum(rsbuf[8 * q : 8 * q + 8, :], axis=0, keepdims=True) for q in range(4)
        ]
        squares = [jnp.sum(raw * raw, axis=1, keepdims=True) for raw in raws]
        mean_sq = (squares[0] + squares[1] + squares[2] + squares[3]) * (1.0 / PROJ)
        scale = lax.rsqrt(mean_sq + 1e-06)
        for q in range(4):
            feat_ref[:, QUART * q : QUART * (q + 1)] = raws[q] * scale

    def mean_half():
        for k in range(1, 4):
            arrive(mrecv.at[(xx + 4 - k) % 4], ms.at[k], mr.at[k])
        mboth[y_hi] = (mrecv[0] + mrecv[1]) + (mrecv[2] + mrecv[3])
        send(mboth.at[y_hi], mboth.at[y_hi], m2s.at[0], m2r.at[0], dev((y + 2) % 4, xx, z, core))

    def mean_done():
        arrive(mboth.at[1 - y_hi], m2s.at[0], m2r.at[0])
        total = mboth[0] + mboth[1]
        total = total * (1.0 / 256.0)
        wsum[...] = total
        pick = jnp.where(
            lax.broadcasted_iota(I32, (128, 8), 0) % 8 == lax.broadcasted_iota(I32, (128, 8), 1), 1.0, 0.0
        ).astype(F32)
        spread = nn(pick, total, precision=lax.Precision.HIGHEST)
        d_at = lax.broadcasted_iota(I32, (128, WIN), 1)
        lane_at = lax.broadcasted_iota(I32, (128, WIN), 0)
        spread = jnp.where(d_at % 16 == lane_at // 8, spread, 0.0)
        d_row = lax.broadcasted_iota(I32, (40, WIN), 1)
        row_at = lax.broadcasted_iota(I32, (40, WIN), 0)
        chosen = jnp.where(d_row // 16 == row_at + 36 * x_lo, 1.0, 0.0).astype(F32)
        flat = nt(chosen, spread, precision=lax.Precision.HIGHEST)
        mean_ref[...] = flat[:36]

        @pl.when((z == 7) & (x_lo == 0))
        def _():
            for row in range(8, 36):
                g = (row - 8) * 128
                r, b = g // 1024, (g % 1024) // 128
                mean_ref[row : row + 1, :] = wsum[r : r + 1, 128 * (b + 1) : 128 * (b + 2)]

        @pl.when((z == 7) & (x_lo == 1))
        def _():
            for row in range(36):
                g = 3584 + row * 128
                r, b = g // 1024, (g % 1024) // 128
                mean_ref[row : row + 1, :] = wsum[r : r + 1, 128 * (b + 1) : 128 * (b + 2)]

    def relay(dz, step):
        z_arrive(0, dz, step)
        z_arrive(1, dz, CHUNKS - 1 - step)

    relay(1, 0)
    sign_units(0, 10)
    relay(1, 1)
    sign_units(10, 18)
    relay(1, 2)
    sign_units(18, 28)
    relay(1, 3)
    pass_on(z, 0)
    tokens_arrive()
    ld_w.wait()
    shard_product(0)
    sign_units(28, 40)
    windows_arrive((1, 7, 2, 6))
    y_arrive(7)
    y_arrive(1)
    relay(2, 0)
    windows_arrive((3, 5, 4))
    c_arrive(7)
    relay(2, 1)
    c_arrive(1)
    relay(2, 2)
    sign_units(40, 48)
    relay(2, 3)
    sign_units(48, 56)
    relay(3, 0)
    stage_three()
    sign_units(56, 64)
    relay(3, 1)
    y_arrive(6)
    y_arrive(2)
    sign_units(64, 72)
    relay(3, 2)
    gather_done()
    c_arrive(6)
    relay(3, 3)
    c_arrive(2)
    relay(4, 0)
    relay(4, 1)
    feature_product()
    y_arrive(5)
    y_arrive(3)
    c_arrive(5)
    y_arrive(4)
    c_arrive(3)
    mean_half()
    c_arrive(4)
    features_done()
    mean_done()
    for e in (0, 7, 1, 6, 2, 5, 3, 4):
        block_arrive(e)

    for copy in sends:
        copy.wait_send()
    for copy in stores:
        copy.wait()


def finish(grads_in, feat_in, mean_in, grads_out, feat_out, mean_out, gbuf, fbuf, mbuf, in_sem, out_sem):
    n = 8
    pieces = [
        (grads_in.at[pl.ds(32 * k, 32), :], gbuf.at[pl.ds(32 * k, 32), :], grads_out.at[pl.ds(32 * k, 32), :])
        for k in range(n)
    ]
    pieces.append((feat_in, fbuf, feat_out))
    pieces.append((mean_in, mbuf, mean_out))
    loads = [pltpu.make_async_copy(p[0], p[1], in_sem.at[k]) for k, p in enumerate(pieces)]
    stores = [pltpu.make_async_copy(p[1], p[2], out_sem.at[k]) for k, p in enumerate(pieces)]
    for load in loads:
        load.start()
    for load, store in zip(loads, stores):
        load.wait()
        store.start()
    for store in stores:
        store.wait()


def per_device(inputs, upstream, value_weight, adapter_in, adapter_out, sign_seed):
    any_spec = pl.BlockSpec(memory_space=pl.ANY)
    vmem_spec = pl.BlockSpec(memory_space=pltpu.VMEM)
    dma = pltpu.SemaphoreType.DMA
    grads, features, mean_grad = pl.pallas_call(
        kernel,
        out_shape=(
            jax.ShapeDtypeStruct((TOK, D), BF16),
            jax.ShapeDtypeStruct((1, PROJ), F32),
            jax.ShapeDtypeStruct((36, 128), F32),
        ),
        in_specs=[
            any_spec, any_spec, any_spec, vmem_spec, vmem_spec,
            pl.BlockSpec(memory_space=pltpu.SMEM),
        ],
        out_specs=(any_spec, vmem_spec, vmem_spec),
        scratch_shapes=[
            pltpu.VMEM((TOK, D), BF16),
            pltpu.VMEM((2 * TOK, KV), BF16),
            pltpu.VMEM((8, SHARD, KV), BF16),
            pltpu.VMEM((8, 2 * TOK, SHARD), BF16),
            pltpu.VMEM((24, D), BF16),
            pltpu.VMEM((2 * TOK, 24), BF16),
            pltpu.VMEM((24, KV), BF16),
            pltpu.VMEM((8, D + KV), BF16),
            pltpu.VMEM((4, 8, 8, WIN), BF16),
            pltpu.VMEM((9, 256, 128), F32),
            pltpu.VMEM((8, 32, WIN), BF16),
            pltpu.VMEM((2, 16, QUART), I32),
            pltpu.VMEM((8, WIN, QUART), BF16),
            pltpu.VMEM((32, QUART), F32),
            pltpu.VMEM((32, QUART), F32),
            pltpu.VMEM((8, WIN), F32),
            pltpu.VMEM((4, 8, WIN), F32),
            pltpu.VMEM((2, 8, WIN), F32),
            pltpu.VMEM((8, WIN), F32),
            dma((6,)), dma((8,)), dma((2,)), dma((2,)),
            dma((2, 4, 4)), dma((2, 4, 4)),
            dma((8, 2, 2)), dma((8, 2, 2)),
            dma((8, 4)), dma((8, 4)),
            dma((8,)), dma((8,)),
            dma((8,)), dma((8,)), dma((8,)), dma((8,)), dma((2, 8)), dma((2, 8)),
            dma((4,)), dma((4,)), dma((1,)), dma((1,)), dma((32,)), dma((32,)),
        ],
        compiler_params=pltpu.CompilerParams(
            collective_id=0, has_side_effects=True, vmem_limit_bytes=64 * 1024 * 1024 - 65536
        ),
    )(inputs, upstream, value_weight, adapter_in.T, adapter_out, sign_seed)
    grads, features, mean_grad = pl.pallas_call(
        finish,
        out_shape=(
            jax.ShapeDtypeStruct((TOK, D), BF16),
            jax.ShapeDtypeStruct((1, PROJ), F32),
            jax.ShapeDtypeStruct((36, 128), F32),
        ),
        in_specs=[any_spec] * 3,
        out_specs=(any_spec,) * 3,
        scratch_shapes=[
            pltpu.VMEM((TOK, D), BF16), pltpu.VMEM((1, PROJ), F32), pltpu.VMEM((36, 128), F32),
            dma((10,)), dma((10,)),
        ],
    )(grads, features, mean_grad)
    return grads, features, mean_grad.reshape(-1)


def solution(mesh):
    return jax.shard_map(
        per_device,
        mesh=mesh,
        in_specs=(
            P(("grp", "fsdp"), None),
            P(("grp", "fsdp"), None),
            P("fsdp", None),
            P(),
            P(),
            P(),
        ),
        out_specs=(P(("grp", "fsdp"), None), P(("grp", "fsdp"), None), P("fsdp")),
        check_vma=False,
    )
```

```python
import jax
import jax.numpy as jnp
from jax import lax
from jax.experimental import pallas as pl
from jax.experimental.pallas import tpu as pltpu
from jax.sharding import PartitionSpec as P

MESH = pl.DeviceIdType.MESH
F32 = jnp.float32
BF16 = jnp.bfloat16
I32 = jnp.int32

D = 8192
KV = 1024
PROJ = 4096
TOK = 256
SHARD = 512
WIN = 1152
NZ = 8
QUART = 1024
CHUNK = 32
CHUNKS = 4
HALF_TOK = 128

ROW_MUL = -1640531535
COL_MUL = -2048144789
SEED_MUL = 668265263
MIX_MUL_4 = 181057748


def nt(left, right, **kw):
    return lax.dot_general(
        left, right, (((1,), (1,)), ((), ())), preferred_element_type=F32, **kw
    )


def nn(left, right, **kw):
    return lax.dot_general(
        left, right, (((1,), (0,)), ((), ())), preferred_element_type=F32, **kw
    )


def kernel(
    x_hbm, u_hbm, w_hbm, ain_ref, aout_ref, seed_ref,
    out_hbm, feat_ref, mean_ref,
    xbuf, ubuf, wbuf, obuf, a3, t3, aout3, pbuf, rx, stage, lhs, hb, signs, acc, rsbuf, msum, mrecv, mboth, wsum,
    ld_sem, st_sem, us, ur, zs, zr, xs, xr, ys, yr, cs, cr, p1s, p1r, p2s, p2r, p3s, p3r, ms, mr, m2s, m2r, rs, rr,
):
    gi = lax.axis_index("grp")
    fi = lax.axis_index("fsdp")
    core = gi % 2
    x_hi = (gi // 2) % 2
    y = gi // 4
    x_lo = fi % 2
    z = fi // 2
    par = y % 2
    y_hi = y // 2
    xx = x_hi * 2 + x_lo

    def dev(y_, x_, z_, c_):
        return ((y_ * 2 + x_ // 2) * 2 + c_, z_ * 2 + x_ % 2)

    z_up, z_dn = dev(y, xx, (z + 1) % 8, core), dev(y, xx, (z + 7) % 8, core)
    x_up, x_dn = dev(y, (xx + 1) % 4, z, core), dev(y, (xx + 3) % 4, z, core)
    y_up, y_dn = dev((y + 1) % 4, xx, z, core), dev((y + 3) % 4, xx, z, core)
    y_mate = dev(y_hi * 2 + (1 - par), xx, z, core)
    c_mate = dev(y, xx, z, 1 - core)

    def member(n):
        k = n // 4
        dz = 4 + ((k + 1) // 2) * (1 - 2 * (k % 2))
        sub = (n + 1) % 4
        return dz, (par + sub // 2) % 2, (core + sub % 2) % 2

    barrier = pltpu.get_barrier_semaphore()

    def signal(target):
        pl.semaphore_signal(barrier, inc=1, device_id=target, device_id_type=MESH)

    def greet(n, carry):
        dz, yt, ct = member(n)
        signal(dev(y_hi * 2 + yt, xx, (z + dz) % 8, ct))
        return carry

    lax.fori_loop(0, 31, greet, 0)
    for k in range(1, 4):
        signal(dev(y, (xx + k) % 4, z, core))
    signal(dev((y + 2) % 4, xx, z, core))
    signal(dev((y + 3 + 2 * par) % 4, xx, z, core))

    ld_u = pltpu.make_async_copy(u_hbm, ubuf.at[pl.ds(0, TOK)], ld_sem.at[0])
    ld_u.start()
    ld_x = []
    for k in range(4):
        cols = pl.ds(2048 * k, 2048)
        ld_x.append(pltpu.make_async_copy(x_hbm.at[:, cols], xbuf.at[:, cols], ld_sem.at[1 + k]))
        ld_x[-1].start()
    ld_w = pltpu.make_async_copy(w_hbm, wbuf.at[z], ld_sem.at[5])
    ld_w.start()

    k0 = QUART * (2 * par + core)
    row16 = lax.broadcasted_iota(I32, (16, QUART), 0)
    col16 = (lax.broadcasted_iota(I32, (16, QUART), 1) + k0) * COL_MUL + seed_ref[0] * SEED_MUL
    hb[0] = row16 * jnp.int32(8) * ROW_MUL + col16
    hb[1] = row16 * ROW_MUL + col16

    def sign_units(first, last):
        @pl.loop(first, last)
        def _(unit):
            r = unit // 9
            blk = unit % 9
            gblk = 9 * z + blk
            is_out = gblk // 64
            i_in = 1024 * gblk + r
            i_out = 65536 - 8192 + 1024 * r + 128 * gblk
            i0 = i_in + is_out * (i_out - i_in)
            step = (8 - 7 * is_out) * 16

            for g in range(8):
                h = hb[is_out] + (i0 + step * g) * ROW_MUL
                h = h ^ lax.shift_right_logical(h, 15)
                h = h * MIX_MUL_4
                h = h ^ (h << 13)
                signs[r, pl.ds(pl.multiple_of(blk * 128 + g * 16, 16), 16), :] = jnp.where(
                    h < 0, -1.0, 1.0
                ).astype(BF16)

    ain = ain_ref[...]
    ain_f = ain.astype(F32)
    a3[...] = jnp.concatenate([ain_f, ain_f, ain_f], axis=0).astype(BF16)
    aout = aout_ref[...]
    aout_f = aout.astype(F32)
    aout3[...] = jnp.concatenate([aout_f, aout_f, aout_f], axis=0).astype(BF16)

    def low_rank(first):
        twice = 2.0 * nt(ubuf[first : first + TOK, :], aout3[...])
        part_hi = twice.astype(BF16).astype(F32)
        rest = twice - part_hi
        part_mid = rest.astype(BF16).astype(F32)
        lane = lax.broadcasted_iota(I32, (TOK, 24), 1)
        t3[first : first + TOK, :] = jnp.where(
            lane < 8, part_hi, jnp.where(lane < 16, part_mid, rest - part_mid)
        ).astype(BF16)

    ld_u.wait()
    scaled = (2.0 * nt(aout, ubuf[:TOK, :])).astype(BF16)

    base = core * 256

    def rows(start, n):
        return pl.ds(pl.multiple_of(start, 16), n)

    def chunk_rows(parity, chunk):
        return rows(base + 128 * parity + CHUNK * chunk, CHUNK)

    def shard_at(e):
        return (z + e) % 8

    sends = []

    def send(src, dst, s_sem, r_sem, target):
        copy = pltpu.make_async_remote_copy(
            src_ref=src, dst_ref=dst, send_sem=s_sem, recv_sem=r_sem,
            device_id=target, device_id_type=MESH,
        )
        copy.start()
        sends.append(copy)

    def arrive(dst, s_sem, r_sem):
        pltpu.make_async_remote_copy(
            src_ref=dst, dst_ref=dst, send_sem=s_sem, recv_sem=r_sem,
            device_id=c_mate, device_id_type=MESH,
        ).wait_recv()

    def z_send(direction, dz, chunk, src, m):
        send(
            src, wbuf.at[m, chunk_rows(par, chunk)], zs.at[direction, dz - 1, chunk],
            zr.at[direction, dz - 1, chunk], z_up if direction == 0 else z_dn,
        )

    def z_arrive(direction, dz, chunk):
        e = (8 - dz) % 8 if direction == 0 else dz
        m = shard_at(e)
        ref = wbuf.at[m, chunk_rows(par, chunk)]
        arrive(ref, zs.at[direction, dz - 1, chunk], zr.at[direction, dz - 1, chunk])
        if dz < 3 or (dz == 3 and chunk // 2 == direction):
            z_send(direction, dz + 1, chunk, ref, m)
        send(ref, ref, ys.at[e, chunk], yr.at[e, chunk], y_up if chunk < 2 else y_dn)

    def y_arrive(e):
        m = shard_at(e)
        for chunk in range(CHUNKS):
            arrive(wbuf.at[m, chunk_rows(1 - par, chunk)], ys.at[e, chunk], yr.at[e, chunk])
        ref = wbuf.at[m, rows(base, 256)]
        send(ref, ref, cs.at[e], cr.at[e], c_mate)

    stores = []

    def block_cols(m, lo, h):
        return pl.ds(pl.multiple_of((m * 2 + lo) * SHARD + h * 256, 256), 256)

    def block_copy(e, h, j):
        start = pl.multiple_of(h * 256, 256)
        return pltpu.make_async_remote_copy(
            src_ref=obuf.at[e, pl.ds(TOK + HALF_TOK * j, HALF_TOK), pl.ds(start, 256)],
            dst_ref=out_hbm.at[pl.ds(HALF_TOK * j, HALF_TOK), block_cols(shard_at(e), x_lo, h)],
            send_sem=xs.at[e, h, j], recv_sem=xr.at[e, h, j],
            device_id=x_up if j else x_dn, device_id_type=MESH,
        )

    def shard_product(e):
        m = shard_at(e)

        @pl.loop(0, 2)
        def _(h):
            start = pl.multiple_of(h * 256, 256)
            cols = block_cols(m, x_lo, h)
            part = nt(ubuf[...], wbuf[m, pl.ds(start, 256), :]) + nn(t3[...], a3[:, cols])
            obuf[e, :, pl.ds(start, 256)] = part.astype(BF16)
            for j in (0, 1):
                block_copy(e, h, j).start()

        cols = pl.ds(pl.multiple_of((m * 2 + x_lo) * SHARD, SHARD), SHARD)
        copy = pltpu.make_async_copy(
            obuf.at[e, pl.ds(0, TOK), :], out_hbm.at[:, cols], st_sem.at[e]
        )
        copy.start()
        stores.append(copy)

    def block_arrive(e):
        m = shard_at(e)
        for h in (0, 1):
            for j in (0, 1):
                rows_j = pl.ds(HALF_TOK * j, HALF_TOK)
                arrive(out_hbm.at[rows_j, block_cols(m, 1 - x_lo, h)], xs.at[e, h, j], xr.at[e, h, j])
                block_copy(e, h, j).wait_send()

    def c_arrive(e):
        arrive(wbuf.at[shard_at(e), rows((1 - core) * 256, 256)], cs.at[e], cr.at[e])
        shard_product(e)

    def tokens_arrive():
        for j in (0, 1):
            arrive(ubuf.at[pl.ds(TOK + HALF_TOK * j, HALF_TOK)], us.at[j], ur.at[j])
        low_rank(TOK)

    pl.semaphore_wait(barrier, 36)

    for j, target in ((0, x_up), (1, x_dn)):
        send(
            ubuf.at[pl.ds(HALF_TOK * j, HALF_TOK)], ubuf.at[pl.ds(TOK + HALF_TOK * j, HALF_TOK)],
            us.at[j], ur.at[j], target,
        )
    for chunk in range(CHUNKS):
        for direction in (0, 1):
            own = chunk if direction == 0 else CHUNKS - 1 - chunk
            z_send(direction, 1, own, w_hbm.at[chunk_rows(par, own)], z)

    narrow = jnp.zeros((8, TOK), F32)
    for k in range(4):
        ld_x[k].wait()
        cols = pl.ds(2048 * k, 2048)
        chunk = xbuf[:, cols]
        pbuf[:, cols] = nn(scaled, chunk).astype(BF16)
        narrow = narrow + nt(ain[:, 2048 * k : 2048 * k + 2048], chunk)
    pbuf[:, pl.ds(D, KV)] = (2.0 * nn(narrow.astype(BF16), ubuf[:TOK, :])).astype(BF16)

    own_blk = par * 2 + core
    mate_blk = (1 - par) * 2 + core
    for dz in (1, 7, 2, 6, 4, 3, 5):
        zt = (z + dz) % 8
        send(
            pbuf.at[:, pl.ds(pl.multiple_of(WIN * zt, 128), WIN)], rx.at[own_blk, z],
            p1s.at[dz], p1r.at[dz], dev(y, xx, zt, core),
        )
    rx[own_blk, z] = pbuf[:, pl.ds(pl.multiple_of(WIN * z, 128), WIN)]
    low_rank(0)

    def pass_on(slot, n):
        ref = rx.at[own_blk, slot]
        send(ref, ref, p2s.at[n], p2r.at[n], y_mate)
        send(ref, ref, p3s.at[0, n], p3r.at[0, n], c_mate)

    def windows_arrive(distances):
        for dz in distances:
            slot = (z + 8 - dz) % 8
            arrive(rx.at[own_blk, slot], p1s.at[dz], p1r.at[dz])
            pass_on(slot, dz)

    def stage_three():
        for dz in range(8):
            ref = rx.at[mate_blk, (z + 8 - dz) % 8]
            arrive(ref, p2s.at[dz], p2r.at[dz])
        send(rx.at[mate_blk], rx.at[mate_blk], p3s.at[1, 0], p3r.at[1, 0], c_mate)

    def gather_done():
        for dz in range(8):
            arrive(rx.at[par * 2 + 1 - core, (z + 8 - dz) % 8], p3s.at[0, dz], p3r.at[0, dz])
        arrive(rx.at[(1 - par) * 2 + 1 - core], p3s.at[1, 0], p3r.at[1, 0])
        msum[...] = jnp.zeros_like(msum)

        @pl.loop(0, 32)
        def _(j):
            block = rx[j // 8, j % 8].astype(F32)
            for b in range(9):
                stage[b, pl.ds(pl.multiple_of(j * 8, 8), 8), :] = block[:, 128 * b : 128 * b + 128]
            msum[...] += block

        mrecv[xx] = msum[...]
        for k in range(1, 4):
            send(msum, mrecv.at[xx], ms.at[k], mr.at[k], dev(y, (xx + k) % 4, z, core))
        for r in range(8):
            for b in range(9):
                lhs[r, :, 128 * b : 128 * b + 128] = stage[b, pl.ds(r, 32, stride=8), :].astype(BF16)

    def feature_product():
        acc[...] = jnp.zeros_like(acc)

        @pl.loop(0, 8)
        def _(r):
            acc[...] += nn(lhs[r], signs[r])

        def row_send(n, carry):
            dz, yt, ct = member(n)
            zt = (z + dz) % 8
            src_row = (yt * 2 + ct) * 8 + zt
            dst_row = (par * 2 + core) * 8 + z
            pltpu.make_async_remote_copy(
                src_ref=acc.at[pl.ds(src_row, 1), :], dst_ref=rsbuf.at[pl.ds(dst_row, 1), :],
                send_sem=rs.at[n], recv_sem=rr.at[n],
                device_id=dev(y_hi * 2 + yt, xx, zt, ct), device_id_type=MESH,
            ).start()
            return carry

        lax.fori_loop(0, 31, row_send, 0)
        own_row = pl.ds(own_blk * 8 + z, 1)
        rsbuf[own_row, :] = acc[own_row, :]

    def row_wait(n, carry):
        dz, yt, ct = member(n)
        row = (yt * 2 + ct) * 8 + (z + 8 - dz) % 8
        ref = rsbuf.at[pl.ds(row, 1), :]
        copy = pltpu.make_async_remote_copy(
            src_ref=ref, dst_ref=ref, send_sem=rs.at[n], recv_sem=rr.at[n],
            device_id=c_mate, device_id_type=MESH,
        )
        copy.wait_recv()
        copy.wait_send()
        return carry

    def features_done():
        lax.fori_loop(0, 31, row_wait, 0)
        raws = [
            jnp.sum(rsbuf[8 * q : 8 * q + 8, :], axis=0, keepdims=True) for q in range(4)
        ]
        squares = [jnp.sum(raw * raw, axis=1, keepdims=True) for raw in raws]
        mean_sq = (squares[0] + squares[1] + squares[2] + squares[3]) * (1.0 / PROJ)
        scale = lax.rsqrt(mean_sq + 1e-06)
        for q in range(4):
            feat_ref[:, QUART * q : QUART * (q + 1)] = raws[q] * scale

    def mean_half():
        for k in range(1, 4):
            arrive(mrecv.at[(xx + 4 - k) % 4], ms.at[k], mr.at[k])
        mboth[y_hi] = (mrecv[0] + mrecv[1]) + (mrecv[2] + mrecv[3])
        send(mboth.at[y_hi], mboth.at[y_hi], m2s.at[0], m2r.at[0], dev((y + 2) % 4, xx, z, core))

    def mean_done():
        arrive(mboth.at[1 - y_hi], m2s.at[0], m2r.at[0])
        total = mboth[0] + mboth[1]
        total = total * (1.0 / 256.0)
        wsum[...] = total
        pick = jnp.where(
            lax.broadcasted_iota(I32, (128, 8), 0) % 8 == lax.broadcasted_iota(I32, (128, 8), 1), 1.0, 0.0
        ).astype(F32)
        spread = nn(pick, total, precision=lax.Precision.HIGHEST)
        d_at = lax.broadcasted_iota(I32, (128, WIN), 1)
        lane_at = lax.broadcasted_iota(I32, (128, WIN), 0)
        spread = jnp.where(d_at % 16 == lane_at // 8, spread, 0.0)
        d_row = lax.broadcasted_iota(I32, (40, WIN), 1)
        row_at = lax.broadcasted_iota(I32, (40, WIN), 0)
        chosen = jnp.where(d_row // 16 == row_at + 36 * x_lo, 1.0, 0.0).astype(F32)
        flat = nt(chosen, spread, precision=lax.Precision.HIGHEST)
        mean_ref[...] = flat[:36]

        @pl.when((z == 7) & (x_lo == 0))
        def _():
            for row in range(8, 36):
                g = (row - 8) * 128
                r, b = g // 1024, (g % 1024) // 128
                mean_ref[row : row + 1, :] = wsum[r : r + 1, 128 * (b + 1) : 128 * (b + 2)]

        @pl.when((z == 7) & (x_lo == 1))
        def _():
            for row in range(36):
                g = 3584 + row * 128
                r, b = g // 1024, (g % 1024) // 128
                mean_ref[row : row + 1, :] = wsum[r : r + 1, 128 * (b + 1) : 128 * (b + 2)]

    def relay(dz, step):
        z_arrive(0, dz, step)
        z_arrive(1, dz, CHUNKS - 1 - step)

    relay(1, 0)
    sign_units(0, 10)
    relay(1, 1)
    sign_units(10, 18)
    relay(1, 2)
    sign_units(18, 28)
    relay(1, 3)
    pass_on(z, 0)
    tokens_arrive()
    ld_w.wait()
    shard_product(0)
    sign_units(28, 40)
    windows_arrive((1, 7, 2, 6, 3, 5))
    y_arrive(7)
    y_arrive(1)
    windows_arrive((4,))
    relay(2, 0)
    c_arrive(7)
    relay(2, 1)
    c_arrive(1)
    relay(2, 2)
    sign_units(40, 48)
    relay(2, 3)
    sign_units(48, 56)
    relay(3, 0)
    stage_three()
    sign_units(56, 64)
    relay(3, 1)
    y_arrive(6)
    y_arrive(2)
    sign_units(64, 72)
    relay(3, 2)
    gather_done()
    c_arrive(6)
    relay(3, 3)
    c_arrive(2)
    relay(4, 0)
    relay(4, 1)
    feature_product()
    y_arrive(5)
    y_arrive(3)
    c_arrive(5)
    y_arrive(4)
    c_arrive(3)
    mean_half()
    c_arrive(4)
    features_done()
    mean_done()
    for e in (0, 7, 1, 6, 2, 5, 3, 4):
        block_arrive(e)

    for copy in sends:
        copy.wait_send()
    for copy in stores:
        copy.wait()


def finish(grads_in, feat_in, mean_in, grads_out, feat_out, mean_out, gbuf, fbuf, mbuf, in_sem, out_sem):
    n = 8
    pieces = [
        (grads_in.at[pl.ds(32 * k, 32), :], gbuf.at[pl.ds(32 * k, 32), :], grads_out.at[pl.ds(32 * k, 32), :])
        for k in range(n)
    ]
    pieces.append((feat_in, fbuf, feat_out))
    pieces.append((mean_in, mbuf, mean_out))
    loads = [pltpu.make_async_copy(p[0], p[1], in_sem.at[k]) for k, p in enumerate(pieces)]
    stores = [pltpu.make_async_copy(p[1], p[2], out_sem.at[k]) for k, p in enumerate(pieces)]
    for load in loads:
        load.start()
    for load, store in zip(loads, stores):
        load.wait()
        store.start()
    for store in stores:
        store.wait()


def per_device(inputs, upstream, value_weight, adapter_in, adapter_out, sign_seed):
    any_spec = pl.BlockSpec(memory_space=pl.ANY)
    vmem_spec = pl.BlockSpec(memory_space=pltpu.VMEM)
    dma = pltpu.SemaphoreType.DMA
    grads, features, mean_grad = pl.pallas_call(
        kernel,
        out_shape=(
            jax.ShapeDtypeStruct((TOK, D), BF16),
            jax.ShapeDtypeStruct((1, PROJ), F32),
            jax.ShapeDtypeStruct((36, 128), F32),
        ),
        in_specs=[
            any_spec, any_spec, any_spec, vmem_spec, vmem_spec,
            pl.BlockSpec(memory_space=pltpu.SMEM),
        ],
        out_specs=(any_spec, vmem_spec, vmem_spec),
        scratch_shapes=[
            pltpu.VMEM((TOK, D), BF16),
            pltpu.VMEM((2 * TOK, KV), BF16),
            pltpu.VMEM((8, SHARD, KV), BF16),
            pltpu.VMEM((8, 2 * TOK, SHARD), BF16),
            pltpu.VMEM((24, D), BF16),
            pltpu.VMEM((2 * TOK, 24), BF16),
            pltpu.VMEM((24, KV), BF16),
            pltpu.VMEM((8, D + KV), BF16),
            pltpu.VMEM((4, 8, 8, WIN), BF16),
            pltpu.VMEM((9, 256, 128), F32),
            pltpu.VMEM((8, 32, WIN), BF16),
            pltpu.VMEM((2, 16, QUART), I32),
            pltpu.VMEM((8, WIN, QUART), BF16),
            pltpu.VMEM((32, QUART), F32),
            pltpu.VMEM((32, QUART), F32),
            pltpu.VMEM((8, WIN), F32),
            pltpu.VMEM((4, 8, WIN), F32),
            pltpu.VMEM((2, 8, WIN), F32),
            pltpu.VMEM((8, WIN), F32),
            dma((6,)), dma((8,)), dma((2,)), dma((2,)),
            dma((2, 4, 4)), dma((2, 4, 4)),
            dma((8, 2, 2)), dma((8, 2, 2)),
            dma((8, 4)), dma((8, 4)),
            dma((8,)), dma((8,)),
            dma((8,)), dma((8,)), dma((8,)), dma((8,)), dma((2, 8)), dma((2, 8)),
            dma((4,)), dma((4,)), dma((1,)), dma((1,)), dma((32,)), dma((32,)),
        ],
        compiler_params=pltpu.CompilerParams(
            collective_id=0, has_side_effects=True, vmem_limit_bytes=64 * 1024 * 1024 - 65536
        ),
    )(inputs, upstream, value_weight, adapter_in.T, adapter_out, sign_seed)
    grads, features, mean_grad = pl.pallas_call(
        finish,
        out_shape=(
            jax.ShapeDtypeStruct((TOK, D), BF16),
            jax.ShapeDtypeStruct((1, PROJ), F32),
            jax.ShapeDtypeStruct((36, 128), F32),
        ),
        in_specs=[any_spec] * 3,
        out_specs=(any_spec,) * 3,
        scratch_shapes=[
            pltpu.VMEM((TOK, D), BF16), pltpu.VMEM((1, PROJ), F32), pltpu.VMEM((36, 128), F32),
            dma((10,)), dma((10,)),
        ],
    )(grads, features, mean_grad)
    return grads, features, mean_grad.reshape(-1)


def solution(mesh):
    return jax.shard_map(
        per_device,
        mesh=mesh,
        in_specs=(
            P(("grp", "fsdp"), None),
            P(("grp", "fsdp"), None),
            P("fsdp", None),
            P(),
            P(),
            P(),
        ),
        out_specs=(P(("grp", "fsdp"), None), P(("grp", "fsdp"), None), P("fsdp")),
        check_vma=False,
    )
```
